32 devices in a mesh: grp: 2 (over y), seq: 4 (over z), fsdp: 2 (over x), tp: 2 (over core).
Axes of the slice: x: 2, y: 2, z: 4, core: 2. Of those that a mesh axis runs over, the one named last changes fastest.
Arguments:
- hidden: bfloat16 [4, 1024, 8192], P(('grp', 'fsdp'), 'seq', 'tp'), parts along dimension 0, may hold values from -480 to 480
- targets: int32 [4, 1024], P(('grp', 'fsdp'), 'seq'), parts along dimension 0, may hold values from 65 to 84, as said below
- perturb_sites: int32 [4, 64], P(('grp', 'fsdp')), parts along dimension 0, may hold values from 0 to 1023, as said below
- labels: int32 [4, 64], P(('grp', 'fsdp')), parts along dimension 0, may hold values from 0 to 1, as said below
- norm_gain: float32 [3, 8192], P(None, 'tp'), may hold values from 0.1 to 1.9
- feature_taps: bfloat16 [2, 3, 3, 8192], P(None, None, None, 'tp'), may hold values from -3.5 to 3.5
- short_taps: bfloat16 [7, 8192], P(None, 'tp'), may hold values from -2.5 to 2.5
- long_taps: bfloat16 [128, 8192], P(('seq', 'fsdp'), 'tp'), may hold values from -0.5 to 0.5
- head_weight: bfloat16 [512, 8192], P(('seq', 'fsdp'), 'tp'), may hold values from -80 to 80
Outputs:
- logprob: float32 [4, 1024], P(('grp', 'fsdp'), 'seq'), parts along dimension 0
- surprise: float32 [4, 64], P(('grp', 'fsdp')), parts along dimension 0
- contrast: float32 [4], P(('grp', 'fsdp')), parts along dimension 0
The draws below stay inside these ranges and needn't reach their ends.
There are 2 independent parts, one for each index of `grp`. The reference program is written for one: setup_inputs(seed, part) draws one part's arguments, and reference() takes and returns one part's arrays. A program takes and returns all parts, laid end to end along the dimension named above; an argument that names none is the same for every part. Nothing has to cross between parts.
Inputs may be any that keep to these rules, and one draw needn't show every extreme that they name: `targets`: each target is the byte code of one of the nucleotides A, C, G, T: 65, 67, 71 or 84. `perturb_sites`: the positions of one genome rise, one in each of 64 equal blocks of the genome; the first is 0 and the last 1023. `labels`: exactly 32 sites of each genome are labelled 1.
All inputs are finite; a program needn't handle non-finite values.
Results may differ from the reference program's by a relative error of at most 0.001.
The reference program's roundings to bfloat16 on the way count: a program that leaves them out, or rounds other values in their place, can miss the bound.
Values may be sent and summed in bfloat16 or wider, within the bound.
A program may use at most 64 MiB of HBM per device.

```python
import math
import jax
import jax.numpy as jnp
from jax import lax

D = 8192
VOCAB = 512
FEAT_TAPS = 3
SE_TAPS = 7
MR_TAPS = 128
SITES = 64
GENOMES = 2
LENGTH = 1024


def draw_hidden(key, part):
    key_base, key_cols, key_rows = jax.random.split(key, 3)
    full_shape = (GENOMES, LENGTH, D)
    channel = jnp.arange(D, dtype=jnp.float32) / D
    base_draw = jnp.clip(jax.random.normal(key_base, full_shape, jnp.float32), -6.0, 6.0)
    profile = 3.0 ** channel
    col_scale = profile * jnp.exp(jax.random.uniform(key_cols, (D,), jnp.float32, 0.0, math.log(2.0)))
    row_scale = jnp.exp(jax.random.uniform(key_rows, (GENOMES, LENGTH, 1), jnp.float32, 0.0, math.log(10.0)))
    return (base_draw * col_scale * row_scale).astype(jnp.bfloat16)


def draw_targets(key, part):
    base_codes = jnp.array([65, 67, 71, 84], dtype=jnp.int32)
    drawn_index = jax.random.randint(key, (GENOMES, LENGTH), 0, 4, dtype=jnp.int32)
    return base_codes[drawn_index]


def draw_perturb_sites(key, part):
    block_len = LENGTH // SITES
    offsets = jax.random.randint(key, (GENOMES, SITES), 0, block_len, dtype=jnp.int32)
    offsets = offsets.at[:, 0].set(0)
    offsets = offsets.at[:, SITES - 1].set(block_len - 1)
    return jnp.arange(SITES, dtype=jnp.int32)[None, :] * block_len + offsets


def draw_labels(key, part):
    scores = jax.random.randint(key, (GENOMES, SITES), 0, 2 ** 20, dtype=jnp.int32) * SITES + jnp.arange(SITES, dtype=jnp.int32)[None, :]
    rank_order = jnp.argsort(jnp.argsort(scores, axis=1, stable=True), axis=1, stable=True)
    return (rank_order < SITES // 2).astype(jnp.int32)


def draw_head_weight(key, part):
    key_main = jax.random.fold_in(key, 0)
    unit_scale = 1.0 / math.sqrt(D)
    main_draw = jnp.clip(jax.random.normal(key_main, (VOCAB, D), jnp.float32), -6.0, 6.0) * 3.0 * unit_scale
    return main_draw.astype(jnp.bfloat16)


def steps_of(key, shape, cuts, low, high):
    gain, own = 1.0, jax.random.fold_in(key, 6)
    for dim, parts in cuts:
        heights = jnp.exp(jax.random.uniform(jax.random.fold_in(own, dim), (parts,), jnp.float32, low / len(cuts), high / len(cuts)))
        gain = gain * jnp.repeat(heights, shape[dim] // parts).reshape([-1 if axis == dim else 1 for axis in range(len(shape))])
    return gain


def centred(key, shape, width, bound, cuts=(), held_as=jnp.bfloat16):
    drawn = width * jax.random.normal(key, shape, jnp.float32)
    if cuts:
        drawn = drawn * steps_of(key, shape, cuts, -0.22, 0.18)
    return jnp.clip(drawn, -bound, bound).astype(held_as)


def setup_inputs(seed: int = 0, part: int = 0) -> dict:
    seeds = jax.random.split(jax.random.key(seed), 10)
    part_splits = jax.random.split(jax.random.fold_in(seeds[9], part), 10)
    hidden = draw_hidden(jax.random.fold_in(jax.random.fold_in(seeds[9], part), 71), part)
    targets = draw_targets(jax.random.fold_in(jax.random.fold_in(seeds[9], part), 71), part)
    perturb_sites = draw_perturb_sites(jax.random.fold_in(jax.random.fold_in(seeds[9], part), 71), part)
    labels = draw_labels(jax.random.fold_in(jax.random.fold_in(seeds[9], part), 71), part)
    norm_gain = jnp.clip(1.0 + 0.18 * jax.random.normal(seeds[4], (3, D), jnp.float32), 0.1, 1.9)
    feature_taps = centred(seeds[5], (2, 3, FEAT_TAPS, D), 0.6, 3.5, ((3, 2),))
    short_taps = centred(seeds[6], (SE_TAPS, D), 0.4, 2.5, ((1, 2),))
    long_taps = centred(seeds[7], (MR_TAPS, D), 0.09, 0.5, ((0, 8), (1, 2)))
    head_weight = draw_head_weight(jax.random.fold_in(seeds[9], 71), part)
    return dict(hidden=hidden, targets=targets, perturb_sites=perturb_sites, labels=labels, norm_gain=norm_gain, feature_taps=feature_taps, short_taps=short_taps, long_taps=long_taps, head_weight=head_weight)


eps = 1e-06

def settle(tensor):
    return lax.optimization_barrier(tensor.astype(jnp.bfloat16))

def causal_valid(signal, filter_taps):
    tap_count = filter_taps.shape[0]
    out_len = signal.shape[0] - tap_count + 1
    wide_taps = filter_taps.astype(jnp.float32)
    total = wide_taps[0] * signal[tap_count - 1:tap_count - 1 + out_len].astype(jnp.float32)
    for lag in range(1, tap_count):
        start = tap_count - 1 - lag
        total = total + wide_taps[lag] * signal[start:start + out_len].astype(jnp.float32)
    return total

def causal_filter(signal, filter_taps):
    tap_count = filter_taps.shape[0]
    padded = jnp.pad(signal, ((tap_count - 1, 0), (0, 0)))
    return causal_valid(padded, filter_taps)

def normalize(residual, gain_row):
    widened = residual.astype(jnp.float32)
    row_power = lax.optimization_barrier(jnp.mean(widened * widened, axis=1, keepdims=True))
    return settle(widened * lax.rsqrt(row_power + eps) * gain_row)

def mixer(residual, gain_row, feature_set, inner_taps):
    normed = normalize(residual, gain_row)
    queries = settle(causal_filter(normed, feature_set[0]))
    key_part = settle(causal_filter(normed, feature_set[1]))
    value_part = settle(causal_filter(normed, feature_set[2]))
    inner_term = settle(key_part.astype(jnp.float32) * value_part.astype(jnp.float32))
    filtered = causal_filter(inner_term, inner_taps)
    return settle(residual.astype(jnp.float32) + queries.astype(jnp.float32) * filtered)

def reference(hidden, targets, perturb_sites, labels, norm_gain, feature_taps, short_taps, long_taps, head_weight):

    def one_genome(genome_pair):
        residual, target_row = genome_pair
        after_short = mixer(residual, norm_gain[0], feature_taps[0], short_taps)
        after_long = mixer(after_short, norm_gain[1], feature_taps[1], long_taps)
        final_norm = normalize(after_long, norm_gain[2])
        logits = jnp.dot(final_norm, head_weight.T, preferred_element_type=jnp.float32)
        row_peak = lax.optimization_barrier(jnp.max(logits, axis=1, keepdims=True))
        log_total = jnp.log(lax.optimization_barrier(jnp.sum(jnp.exp(logits - row_peak), axis=1))) + row_peak[:, 0]
        chosen = jnp.take_along_axis(logits, target_row[:, None].astype(jnp.int32), axis=1)[:, 0]
        return chosen - log_total
    logprob = lax.map(one_genome, (hidden, targets))
    running = jnp.cumsum(logprob, axis=1)
    before_all = jnp.concatenate([jnp.zeros((logprob.shape[0], 1), jnp.float32), running[:, :-1]], axis=1)
    prefix_sum = jnp.take_along_axis(before_all, perturb_sites.astype(jnp.int32), axis=1)
    site_logprob = jnp.take_along_axis(logprob, perturb_sites.astype(jnp.int32), axis=1)
    prefix_len = jnp.maximum(perturb_sites, 1).astype(jnp.float32)
    surprise = site_logprob - prefix_sum / prefix_len
    label_sign = (2 * labels - 1).astype(jnp.float32)
    contrast = lax.optimization_barrier(jnp.sum(label_sign * surprise, axis=1)) / (SITES // 2)
    return (logprob, surprise, contrast)
```

```python
import functools

import jax
import jax.numpy as jnp
import numpy as np
from jax import lax
from jax.experimental import pallas as pl
from jax.experimental.pallas import tpu as pltpu
from jax.sharding import PartitionSpec as P

D = 8192
FEAT_TAPS = 3
SE_TAPS = 7
MR_TAPS = 128
SITES = 64


eps = 1e-06


def passed_along(shard, axis, by):
    devices = lax.axis_size(axis)
    pairs = [(i, i + by) for i in range(devices) if 0 <= i + by < devices]
    return lax.ppermute(shard, axis, pairs)


def settle(tensor):
    return lax.optimization_barrier(tensor.astype(jnp.bfloat16))


def split_parts(matrix, parts):
    pieces, left = [], np.asarray(matrix, np.float64)
    for _ in range(parts):
        piece = left.astype(jnp.bfloat16)
        pieces.append(piece)
        left = left - piece.astype(np.float64)
    return np.stack(pieces)


def transform_pair(window, taps):
    half = window // 2
    t = np.arange(window)
    f = np.arange(half)
    angle = 2.0 * np.pi * ((f[:, None] * t[None, :]) % window) / window
    cos_rows, sin_rows = np.cos(angle), np.sin(angle)
    sin_rows[0] = np.where(t % 2 == 0, 1.0, -1.0)
    forward = np.concatenate([cos_rows, sin_rows], axis=0)
    weight = np.full((half,), 2.0 / window)
    weight[0] = 1.0 / window
    inverse = (forward * np.concatenate([weight, weight])[:, None]).T[taps:]
    return split_parts(forward, PARTS), split_parts(inverse, PARTS)


PARTS = 3
CHUNK = 32
WIDTH = 256


def wide(value):
    return value.astype(jnp.float32)


def rounded(value):
    return value.astype(jnp.bfloat16).astype(jnp.float32)


def tap_sum(ref, start, rows, taps):
    total = taps[0] * ref[start : start + rows, :]
    for lag in range(1, len(taps)):
        total = total + taps[lag] * ref[start - lag : start - lag + rows, :]
    return total


def feature_rows(feat_ref, which):
    return [feat_ref[which * FEAT_TAPS + lag : which * FEAT_TAPS + lag + 1, :] for lag in range(FEAT_TAPS)]


def square_lanes(value):
    square = value * value
    total = square[:, :128]
    for at in range(128, square.shape[1], 128):
        total = total + square[:, at : at + 128]
    return total


def short_kernel(hid_ref, rim_ref, scale_ref, gain_ref, feat_ref, taps_ref, out_ref, pow_ref, ext, inner):
    rows = hid_ref.shape[0]
    lead = rim_ref.shape[0]
    tap_count = taps_ref.shape[0]

    @pl.when(pl.program_id(0) == 0)
    def _():
        pow_ref[...] = jnp.zeros_like(pow_ref)

    ext[0:lead, :] = jnp.zeros((lead, ext.shape[1]), jnp.float32)
    ext[lead : 2 * lead, :] = wide(rim_ref[...])
    gain = gain_ref[...]
    for at in range(0, rows, CHUNK):
        block = wide(hid_ref[at : at + CHUNK, :])
        ext[2 * lead + at : 2 * lead + at + CHUNK, :] = rounded(block * scale_ref[at : at + CHUNK, :] * gain)
    k_taps, v_taps = feature_rows(feat_ref, 1), feature_rows(feat_ref, 2)

    def inner_rows(at, count):
        keys = rounded(tap_sum(ext, lead + at, count, k_taps))
        values = rounded(tap_sum(ext, lead + at, count, v_taps))
        inner[at : at + count, :] = rounded(keys * values)

    inner_rows(0, lead)
    for at in range(0, rows, CHUNK):
        inner_rows(lead + at, CHUNK)
    q_taps = feature_rows(feat_ref, 0)
    short = [taps_ref[lag : lag + 1, :] for lag in range(tap_count)]
    for at in range(0, rows, CHUNK):
        queries = rounded(tap_sum(ext, 2 * lead + at, CHUNK, q_taps))
        filtered = tap_sum(inner, lead + at, CHUNK, short)
        result = (wide(hid_ref[at : at + CHUNK, :]) + queries * filtered).astype(jnp.bfloat16)
        out_ref[at : at + CHUNK, :] = result
        pow_ref[at : at + CHUNK, :] += square_lanes(wide(result))


def short_mixer(residual, rim, scale, gain_row, features, taps):
    rows, channels = residual.shape
    lead = rim.shape[0]
    column = lambda i: (0, i)
    fixed = lambda i: (0, 0)
    return pl.pallas_call(
        short_kernel,
        grid=(channels // WIDTH,),
        in_specs=[
            pl.BlockSpec((rows, WIDTH), column),
            pl.BlockSpec((lead, WIDTH), column),
            pl.BlockSpec((rows, 1), fixed),
            pl.BlockSpec((1, WIDTH), column),
            pl.BlockSpec((features.shape[0], WIDTH), column),
            pl.BlockSpec((taps.shape[0], WIDTH), column),
        ],
        out_specs=[pl.BlockSpec((rows, WIDTH), column), pl.BlockSpec((rows, 128), fixed)],
        out_shape=[
            jax.ShapeDtypeStruct((rows, channels), jnp.bfloat16),
            jax.ShapeDtypeStruct((rows, 128), jnp.float32),
        ],
        scratch_shapes=[
            pltpu.VMEM((2 * lead + rows, WIDTH), jnp.float32),
            pltpu.VMEM((lead + rows, WIDTH), jnp.float32),
        ],
        name="short_mixer",
    )(residual, rim, scale, gain_row, features, taps)


def long_kernel(
    res_ref, rim_ref, scale_ref, gain_ref, feat_ref, taps_ref, fwd_ref, inv_ref,
    out_ref, pow_ref, ext, inner, spec_u, spec_w, spec_y, filt,
):
    rows = res_ref.shape[0]
    tap_count = taps_ref.shape[0]
    lead = rim_ref.shape[0]
    window = tap_count + rows
    half = window // 2

    @pl.when(pl.program_id(0) == 0)
    def _():
        pow_ref[...] = jnp.zeros_like(pow_ref)

    ext[0:lead, :] = wide(rim_ref[...])
    gain = gain_ref[...]
    for at in range(0, rows, CHUNK):
        block = wide(res_ref[at : at + CHUNK, :])
        ext[lead + at : lead + at + CHUNK, :] = rounded(block * scale_ref[at : at + CHUNK, :] * gain)
    k_taps, v_taps = feature_rows(feat_ref, 1), feature_rows(feat_ref, 2)
    first = lead - tap_count
    for at in range(0, window, CHUNK):
        keys = rounded(tap_sum(ext, first + at, CHUNK, k_taps))
        values = rounded(tap_sum(ext, first + at, CHUNK, v_taps))
        inner[at : at + CHUNK, :] = (keys * values).astype(jnp.bfloat16)

    def product(left, right):
        return jnp.dot(left, right, preferred_element_type=jnp.float32)

    def forward_of(value, depth):
        total = product(fwd_ref[PARTS - 1][:, :depth], value)
        for part in range(PARTS - 2, -1, -1):
            total = total + product(fwd_ref[part][:, :depth], value)
        return total

    taps = taps_ref[...]
    signal = inner[...]
    spec_w[...] = forward_of(taps, tap_count)
    spec_u[...] = forward_of(signal, window)
    for at in range(0, half, CHUNK):
        lo, hi = slice(at, at + CHUNK), slice(half + at, half + at + CHUNK)
        uc, us, wc, ws = spec_u[lo, :], spec_u[hi, :], spec_w[lo, :], spec_w[hi, :]
        cc, ss = uc * wc, us * ws
        yc, ys = cc - ss, uc * ws + us * wc
        if at == 0:
            is_first = lax.broadcasted_iota(jnp.int32, cc.shape, 0) == 0
            yc, ys = jnp.where(is_first, cc, yc), jnp.where(is_first, ss, ys)
        for rows_at, value in ((lo, yc), (hi, ys)):
            for part in range(PARTS):
                top = value.astype(jnp.bfloat16)
                spec_y[part, rows_at, :] = top
                value = value - wide(top)
    total = None
    for order in range(PARTS - 1, -1, -1):
        for part in range(order + 1):
            term = product(inv_ref[part], spec_y[order - part])
            total = term if total is None else total + term
    filt[...] = total
    q_taps = feature_rows(feat_ref, 0)
    for at in range(0, rows, CHUNK):
        queries = rounded(tap_sum(ext, lead + at, CHUNK, q_taps))
        result = (wide(res_ref[at : at + CHUNK, :]) + queries * filt[at : at + CHUNK, :]).astype(jnp.bfloat16)
        out_ref[at : at + CHUNK, :] = result
        pow_ref[at : at + CHUNK, :] += square_lanes(wide(result))


def long_mixer(residual, rim, scale, gain_row, features, taps):
    rows, channels = residual.shape
    lead, tap_count = rim.shape[0], taps.shape[0]
    window = rows + tap_count
    forward, inverse = transform_pair(window, tap_count)
    column = lambda i: (0, i)
    fixed = lambda i: (0, 0)
    whole = lambda i: (0, 0, 0)
    return pl.pallas_call(
        long_kernel,
        grid=(channels // WIDTH,),
        in_specs=[
            pl.BlockSpec((rows, WIDTH), column),
            pl.BlockSpec((lead, WIDTH), column),
            pl.BlockSpec((rows, 1), fixed),
            pl.BlockSpec((1, WIDTH), column),
            pl.BlockSpec((features.shape[0], WIDTH), column),
            pl.BlockSpec((tap_count, WIDTH), column),
            pl.BlockSpec(forward.shape, whole),
            pl.BlockSpec(inverse.shape, whole),
        ],
        out_specs=[pl.BlockSpec((rows, WIDTH), column), pl.BlockSpec((rows, 128), fixed)],
        out_shape=[
            jax.ShapeDtypeStruct((rows, channels), jnp.bfloat16),
            jax.ShapeDtypeStruct((rows, 128), jnp.float32),
        ],
        scratch_shapes=[
            pltpu.VMEM((lead + rows, WIDTH), jnp.float32),
            pltpu.VMEM((window, WIDTH), jnp.bfloat16),
            pltpu.VMEM((window, WIDTH), jnp.float32),
            pltpu.VMEM((window, WIDTH), jnp.float32),
            pltpu.VMEM((PARTS, window, WIDTH), jnp.bfloat16),
            pltpu.VMEM((rows, WIDTH), jnp.float32),
        ],
        name="long_mixer",
    )(residual, rim, scale, gain_row, features, taps, jnp.asarray(forward), jnp.asarray(inverse))


def row_scale(row_power):
    other = lax.ppermute(row_power, "tp", [(0, 1), (1, 0)])
    return lax.rsqrt((row_power + other) / D + eps)


def scaled_rows(residual, scale_rows, gain_row):
    return settle(residual.astype(jnp.float32) * scale_rows[:, None] * gain_row)


def spread_kernel(count, mine_ref, all_ref, send_sem, recv_sem):
    me = lax.axis_index("seq")
    barrier = pltpu.get_barrier_semaphore()
    for step in range(1, count):
        peer = lax.rem(me + step, count)
        pl.semaphore_signal(barrier, inc=1, device_id={"seq": peer}, device_id_type=pl.DeviceIdType.MESH)
    pl.semaphore_wait(barrier, count - 1)
    copies = []
    for step in range(1, count):
        peer = lax.rem(me + step, count)
        copy = pltpu.make_async_remote_copy(
            src_ref=mine_ref,
            dst_ref=all_ref.at[me],
            send_sem=send_sem.at[step],
            recv_sem=recv_sem.at[step],
            device_id={"seq": peer},
            device_id_type=pl.DeviceIdType.MESH,
        )
        copy.start()
        copies.append(copy)
    all_ref[me] = mine_ref[...]
    for copy in copies:
        copy.wait()


def spread(value):
    count = lax.axis_size("seq")
    return pl.pallas_call(
        functools.partial(spread_kernel, count),
        out_shape=jax.ShapeDtypeStruct((count, *value.shape), value.dtype),
        in_specs=[pl.BlockSpec(memory_space=pltpu.VMEM)],
        out_specs=pl.BlockSpec(memory_space=pltpu.VMEM),
        scratch_shapes=[pltpu.SemaphoreType.DMA((count,)), pltpu.SemaphoreType.DMA((count,))],
        compiler_params=pltpu.CompilerParams(collective_id=0, has_side_effects=True),
        name="spread",
    )(value)


def shards(
    hidden,
    targets,
    perturb_sites,
    labels,
    norm_gain,
    feature_taps,
    short_taps,
    long_taps,
    head_weight,
):
    residual = hidden[0]
    row_count = residual.shape[0]
    short_back = FEAT_TAPS + SE_TAPS - 2
    long_back = FEAT_TAPS + MR_TAPS - 2
    long_lead = -(-long_back // 8) * 8
    widened = residual.astype(jnp.float32)
    scale_one = row_scale(jnp.sum(widened * widened, axis=1))
    last = row_count - short_back
    rim_rows = passed_along(scaled_rows(residual[last:], scale_one[last:], norm_gain[0]), "seq", 1)
    features = feature_taps.astype(jnp.float32).reshape(2, 3 * FEAT_TAPS, -1)
    after_short, power_two = short_mixer(
        residual, rim_rows, scale_one[:, None], norm_gain[0:1], features[0], short_taps.astype(jnp.float32)
    )
    scale_two = row_scale(jnp.sum(power_two, axis=1))
    last = row_count - long_back
    rim_long = passed_along(scaled_rows(after_short[last:], scale_two[last:], norm_gain[1]), "seq", 1)
    rim_long = jnp.pad(rim_long, ((long_lead - long_back, 0), (0, 0)))
    taps_all = lax.all_gather(long_taps, ("seq", "fsdp"), axis=0, tiled=True)
    after_long, power_three = long_mixer(
        after_short, rim_long, scale_two[:, None], norm_gain[1:2], features[1], taps_all
    )
    final_norm = scaled_rows(after_long, row_scale(jnp.sum(power_three, axis=1)), norm_gain[2])
    row_contract = (((1,), (1,)), ((), ()))
    logits_part = lax.dot_general(
        final_norm,
        lax.all_gather(head_weight, ("seq", "fsdp"), axis=0, tiled=True),
        row_contract,
        preferred_element_type=jnp.float32,
    )
    core = lax.axis_index("tp")
    swap = [(0, 1), (1, 0)]
    half_rows = row_count // 2
    kept = lax.dynamic_slice_in_dim(logits_part, core * half_rows, half_rows, 0)
    given = lax.dynamic_slice_in_dim(logits_part, (1 - core) * half_rows, half_rows, 0)
    logits = kept + lax.ppermute(given, "tp", swap)
    row_peak = jnp.max(logits, axis=1, keepdims=True)
    log_total = jnp.log(jnp.sum(jnp.exp(logits - row_peak), axis=1)) + row_peak[:, 0]
    target_row = lax.dynamic_slice_in_dim(targets[0], core * half_rows, half_rows, 0)
    vocab_ids = lax.broadcasted_iota(jnp.int32, logits.shape, 1)
    chosen = jnp.sum(jnp.where(vocab_ids == target_row[:, None], logits, 0.0), axis=1)
    mine = chosen - log_total
    theirs = lax.ppermute(mine, "tp", swap)
    logprob = jnp.where(core == 0, jnp.concatenate([mine, theirs]), jnp.concatenate([theirs, mine]))
    site_row = perturb_sites[0]
    genome_row = spread(logprob.reshape(-1, 128)).reshape(-1)
    positions = lax.broadcasted_iota(jnp.int32, (site_row.shape[0], genome_row.shape[0]), 1)
    prefix_sum = jnp.sum(jnp.where(positions < site_row[:, None], genome_row[None, :], 0.0), axis=1)
    site_logprob = jnp.sum(jnp.where(positions == site_row[:, None], genome_row[None, :], 0.0), axis=1)
    prefix_len = jnp.maximum(site_row, 1).astype(jnp.float32)
    surprise = site_logprob - prefix_sum / prefix_len
    label_sign = (2 * labels[0] - 1).astype(jnp.float32)
    contrast = jnp.sum(label_sign * surprise) / (SITES // 2)
    return (logprob[None, :], surprise[None, :], jnp.reshape(contrast, (1,)))


def solution(mesh):
    placed = (
        P(("grp", "fsdp"), "seq", "tp"),
        P(("grp", "fsdp"), "seq"),
        P(("grp", "fsdp"), None),
        P(("grp", "fsdp"), None),
        P(None, "tp"),
        P(None, None, None, "tp"),
        P(None, "tp"),
        P(("seq", "fsdp"), "tp"),
        P(("seq", "fsdp"), "tp"),
    )
    return jax.shard_map(
        shards,
        mesh=mesh,
        in_specs=placed,
        out_specs=(P(("grp", "fsdp"), "seq"), P(("grp", "fsdp"), None), P(("grp", "fsdp"))),
        check_vma=False,
    )
```

```python
import functools

import jax
import jax.numpy as jnp
import numpy as np
from jax import lax
from jax.experimental import pallas as pl
from jax.experimental.pallas import tpu as pltpu
from jax.sharding import PartitionSpec as P

D = 8192
FEAT_TAPS = 3
SE_TAPS = 7
MR_TAPS = 128
SITES = 64


eps = 1e-06


def passed_along(shard, axis, by):
    devices = lax.axis_size(axis)
    pairs = [(i, i + by) for i in range(devices) if 0 <= i + by < devices]
    return lax.ppermute(shard, axis, pairs)


def settle(tensor):
    return lax.optimization_barrier(tensor.astype(jnp.bfloat16))


def split_parts(matrix, parts):
    pieces, left = [], np.asarray(matrix, np.float64)
    for _ in range(parts):
        piece = left.astype(jnp.bfloat16)
        pieces.append(piece)
        left = left - piece.astype(np.float64)
    return np.stack(pieces)


def transform_pair(window, taps):
    half = window // 2
    t = np.arange(window)
    f = np.arange(half)
    angle = 2.0 * np.pi * ((f[:, None] * t[None, :]) % window) / window
    cos_rows, sin_rows = np.cos(angle), np.sin(angle)
    sin_rows[0] = np.where(t % 2 == 0, 1.0, -1.0)
    forward = np.concatenate([cos_rows, sin_rows], axis=0)
    weight = np.full((half,), 2.0 / window)
    weight[0] = 1.0 / window
    inverse = (forward * np.concatenate([weight, weight])[:, None]).T[taps:]
    return split_parts(forward, PARTS), split_parts(inverse, PARTS)


PARTS = 3
CHUNK = 32
WIDTH = 256


def wide(value):
    return value.astype(jnp.float32)


def rounded(value):
    return value.astype(jnp.bfloat16).astype(jnp.float32)


def tap_sum(ref, start, rows, taps):
    total = taps[0] * ref[start : start + rows, :]
    for lag in range(1, len(taps)):
        total = total + taps[lag] * ref[start - lag : start - lag + rows, :]
    return total


def tap_rows(taps):
    taps = wide(taps)
    return [taps[lag : lag + 1, :] for lag in range(taps.shape[0])]


def feature_rows(feat_ref, which):
    return tap_rows(feat_ref[0, which])


def square_lanes(value):
    square = value * value
    total = square[:, :128]
    for at in range(128, square.shape[1], 128):
        total = total + square[:, at : at + 128]
    return total


def gather_peer(step, counts):
    outer, inner = counts
    place = lax.rem(lax.axis_index("seq") * inner + lax.axis_index("fsdp") + step, outer * inner)
    return place, {"seq": place // inner, "fsdp": lax.rem(place, inner)}


def short_kernel(
    counts, hid_ref, rim_ref, scale_ref, gain_ref, feat_ref, taps_ref, piece_ref,
    out_ref, pow_ref, whole_ref, ext, inner, send_sem, recv_sem, own_sem,
):
    rows = hid_ref.shape[0]
    lead = rim_ref.shape[0]
    holders = counts[0] * counts[1]
    mine, _ = gather_peer(0, counts)

    def to_peer(step):
        _, where = gather_peer(step, counts)
        return pltpu.make_async_remote_copy(
            src_ref=piece_ref,
            dst_ref=whole_ref.at[mine],
            send_sem=send_sem.at[step],
            recv_sem=recv_sem.at[step],
            device_id=where,
            device_id_type=pl.DeviceIdType.MESH,
        )

    own_copy = pltpu.make_async_copy(piece_ref, whole_ref.at[mine], own_sem)

    @pl.when(pl.program_id(0) == 0)
    def _():
        pow_ref[...] = jnp.zeros_like(pow_ref)
        barrier = pltpu.get_barrier_semaphore()

        def greet(step, carry):
            _, where = gather_peer(step, counts)
            pl.semaphore_signal(barrier, inc=1, device_id=where, device_id_type=pl.DeviceIdType.MESH)
            return carry

        def send(step, carry):
            to_peer(step).start()
            return carry

        lax.fori_loop(1, holders, greet, 0)
        pl.semaphore_wait(barrier, holders - 1)
        lax.fori_loop(1, holders, send, 0)
        own_copy.start()

    @pl.when(pl.program_id(0) == pl.num_programs(0) - 1)
    def _():
        def settle_copy(step, carry):
            to_peer(step).wait()
            return carry

        lax.fori_loop(1, holders, settle_copy, 0)
        own_copy.wait()

    ext[0:lead, :] = jnp.zeros((lead, ext.shape[1]), jnp.float32)
    ext[lead : 2 * lead, :] = wide(rim_ref[...])
    gain = gain_ref[0:1, :]
    for at in range(0, rows, CHUNK):
        block = wide(hid_ref[at : at + CHUNK, :])
        ext[2 * lead + at : 2 * lead + at + CHUNK, :] = rounded(block * scale_ref[at : at + CHUNK, :] * gain)
    k_taps, v_taps = feature_rows(feat_ref, 1), feature_rows(feat_ref, 2)

    def inner_rows(at, count):
        keys = rounded(tap_sum(ext, lead + at, count, k_taps))
        values = rounded(tap_sum(ext, lead + at, count, v_taps))
        inner[at : at + count, :] = rounded(keys * values)

    inner_rows(0, lead)
    for at in range(0, rows, CHUNK):
        inner_rows(lead + at, CHUNK)
    q_taps = feature_rows(feat_ref, 0)
    short = tap_rows(taps_ref[...])
    for at in range(0, rows, CHUNK):
        queries = rounded(tap_sum(ext, 2 * lead + at, CHUNK, q_taps))
        filtered = tap_sum(inner, lead + at, CHUNK, short)
        result = (wide(hid_ref[at : at + CHUNK, :]) + queries * filtered).astype(jnp.bfloat16)
        out_ref[at : at + CHUNK, :] = result
        pow_ref[at : at + CHUNK, :] += square_lanes(wide(result))


def short_mixer(residual, rim, scale, gains, features, taps, piece):
    rows, channels = residual.shape
    lead = rim.shape[0]
    counts = (lax.axis_size("seq"), lax.axis_size("fsdp"))
    holders = counts[0] * counts[1]
    column = lambda i: (0, i)
    fixed = lambda i: (0, 0)
    return pl.pallas_call(
        functools.partial(short_kernel, counts),
        grid=(channels // WIDTH,),
        in_specs=[
            pl.BlockSpec((rows, WIDTH), column),
            pl.BlockSpec((lead, WIDTH), column),
            pl.BlockSpec((rows, 1), fixed),
            pl.BlockSpec((gains.shape[0], WIDTH), column),
            pl.BlockSpec((1, *features.shape[1:3], WIDTH), lambda i: (0, 0, 0, i)),
            pl.BlockSpec((taps.shape[0], WIDTH), column),
            pl.BlockSpec(memory_space=pl.ANY),
        ],
        out_specs=[
            pl.BlockSpec((rows, WIDTH), column),
            pl.BlockSpec((rows, 128), fixed),
            pl.BlockSpec(memory_space=pl.ANY),
        ],
        out_shape=[
            jax.ShapeDtypeStruct((rows, channels), jnp.bfloat16),
            jax.ShapeDtypeStruct((rows, 128), jnp.float32),
            jax.ShapeDtypeStruct((holders, *piece.shape), piece.dtype),
        ],
        scratch_shapes=[
            pltpu.VMEM((2 * lead + rows, WIDTH), jnp.float32),
            pltpu.VMEM((lead + rows, WIDTH), jnp.float32),
            pltpu.SemaphoreType.DMA((holders,)),
            pltpu.SemaphoreType.DMA((holders,)),
            pltpu.SemaphoreType.DMA,
        ],
        compiler_params=pltpu.CompilerParams(collective_id=1, has_side_effects=True),
        name="short_mixer",
    )(residual, rim, scale, gains, features, taps, piece)


def long_kernel(
    count, res_ref, edge_ref, scale_ref, gain_ref, feat_ref, taps_ref, fwd_ref, inv_ref,
    out_ref, pow_ref, ext, inner, spec_u, spec_w, spec_y, filt, rim, send_sem, recv_sem,
):
    rows = res_ref.shape[0]
    tap_count = taps_ref.shape[0]
    lead = rim.shape[1]
    step = pl.program_id(0)
    blocks = pl.num_programs(0)
    me = lax.axis_index("seq")
    sends, receives = me < count - 1, me > 0

    def onward(block):
        return pltpu.make_async_remote_copy(
            src_ref=edge_ref.at[:, pl.ds(pl.multiple_of(block * WIDTH, WIDTH), WIDTH)],
            dst_ref=rim.at[block],
            send_sem=send_sem.at[block],
            recv_sem=recv_sem.at[block],
            device_id={"seq": lax.rem(me + 1, count)},
            device_id_type=pl.DeviceIdType.MESH,
        )

    @pl.when(step == 0)
    def _():
        barrier = pltpu.get_barrier_semaphore()

        @pl.when(receives)
        def _():
            pl.semaphore_signal(barrier, inc=1, device_id={"seq": me - 1}, device_id_type=pl.DeviceIdType.MESH)

        @pl.when(sends)
        def _():
            pl.semaphore_signal(barrier, inc=1, device_id={"seq": me + 1}, device_id_type=pl.DeviceIdType.MESH)

        between = jnp.logical_and(receives, sends)

        @pl.when(between)
        def _():
            pl.semaphore_wait(barrier, 2)

        @pl.when(jnp.logical_not(between))
        def _():
            pl.semaphore_wait(barrier, 1)

        @pl.when(sends)
        def _():
            def send(block, carry):
                onward(block).start()
                return carry

            lax.fori_loop(0, blocks, send, 0)

    @pl.when(receives)
    def _():
        onward(step).wait_recv()
        ext[0:lead, :] = wide(rim[step])

    @pl.when(jnp.logical_not(receives))
    def _():
        ext[0:lead, :] = jnp.zeros((lead, ext.shape[1]), jnp.float32)

    @pl.when(sends)
    def _():
        onward(step).wait_send()

    window = tap_count + rows
    half = window // 2

    @pl.when(pl.program_id(0) == 0)
    def _():
        pow_ref[...] = jnp.zeros_like(pow_ref)

    gain = gain_ref[1:2, :]
    for at in range(0, rows, CHUNK):
        block = wide(res_ref[at : at + CHUNK, :])
        ext[lead + at : lead + at + CHUNK, :] = rounded(block * scale_ref[at : at + CHUNK, :] * gain)
    k_taps, v_taps = feature_rows(feat_ref, 1), feature_rows(feat_ref, 2)
    first = lead - tap_count
    for at in range(0, window, CHUNK):
        keys = rounded(tap_sum(ext, first + at, CHUNK, k_taps))
        values = rounded(tap_sum(ext, first + at, CHUNK, v_taps))
        inner[at : at + CHUNK, :] = (keys * values).astype(jnp.bfloat16)

    def product(left, right):
        return jnp.dot(left, right, preferred_element_type=jnp.float32)

    def forward_of(value, depth):
        total = product(fwd_ref[PARTS - 1][:, :depth], value)
        for part in range(PARTS - 2, -1, -1):
            total = total + product(fwd_ref[part][:, :depth], value)
        return total

    taps = taps_ref[...]
    signal = inner[...]
    spec_w[...] = forward_of(taps, tap_count)
    spec_u[...] = forward_of(signal, window)
    for at in range(0, half, CHUNK):
        lo, hi = slice(at, at + CHUNK), slice(half + at, half + at + CHUNK)
        uc, us, wc, ws = spec_u[lo, :], spec_u[hi, :], spec_w[lo, :], spec_w[hi, :]
        cc, ss = uc * wc, us * ws
        yc, ys = cc - ss, uc * ws + us * wc
        if at == 0:
            is_first = lax.broadcasted_iota(jnp.int32, cc.shape, 0) == 0
            yc, ys = jnp.where(is_first, cc, yc), jnp.where(is_first, ss, ys)
        for rows_at, value in ((lo, yc), (hi, ys)):
            for part in range(PARTS):
                top = value.astype(jnp.bfloat16)
                spec_y[part, rows_at, :] = top
                value = value - wide(top)
    total = None
    for order in range(PARTS - 1, -1, -1):
        for part in range(order + 1):
            term = product(inv_ref[part], spec_y[order - part])
            total = term if total is None else total + term
    filt[...] = total
    q_taps = feature_rows(feat_ref, 0)
    for at in range(0, rows, CHUNK):
        queries = rounded(tap_sum(ext, lead + at, CHUNK, q_taps))
        result = (wide(res_ref[at : at + CHUNK, :]) + queries * filt[at : at + CHUNK, :]).astype(jnp.bfloat16)
        out_ref[at : at + CHUNK, :] = result
        pow_ref[at : at + CHUNK, :] += square_lanes(wide(result))


def long_mixer(residual, edge, scale, gains, features, taps):
    rows, channels = residual.shape
    lead, tap_count = edge.shape[0], taps.shape[0]
    count, blocks = lax.axis_size("seq"), channels // WIDTH
    window = rows + tap_count
    forward, inverse = transform_pair(window, tap_count)
    column = lambda i: (0, i)
    fixed = lambda i: (0, 0)
    whole = lambda i: (0, 0, 0)
    return pl.pallas_call(
        functools.partial(long_kernel, count),
        grid=(channels // WIDTH,),
        in_specs=[
            pl.BlockSpec((rows, WIDTH), column),
            pl.BlockSpec(memory_space=pl.ANY),
            pl.BlockSpec((rows, 1), fixed),
            pl.BlockSpec((gains.shape[0], WIDTH), column),
            pl.BlockSpec((1, *features.shape[1:3], WIDTH), lambda i: (1, 0, 0, i)),
            pl.BlockSpec((tap_count, WIDTH), column),
            pl.BlockSpec(forward.shape, whole),
            pl.BlockSpec(inverse.shape, whole),
        ],
        out_specs=[pl.BlockSpec((rows, WIDTH), column), pl.BlockSpec((rows, 128), fixed)],
        out_shape=[
            jax.ShapeDtypeStruct((rows, channels), jnp.bfloat16),
            jax.ShapeDtypeStruct((rows, 128), jnp.float32),
        ],
        scratch_shapes=[
            pltpu.VMEM((lead + rows, WIDTH), jnp.float32),
            pltpu.VMEM((window, WIDTH), jnp.bfloat16),
            pltpu.VMEM((window, WIDTH), jnp.float32),
            pltpu.VMEM((window, WIDTH), jnp.float32),
            pltpu.VMEM((PARTS, window, WIDTH), jnp.bfloat16),
            pltpu.VMEM((rows, WIDTH), jnp.float32),
            pltpu.VMEM((blocks, lead, WIDTH), jnp.bfloat16),
            pltpu.SemaphoreType.DMA((blocks,)),
            pltpu.SemaphoreType.DMA((blocks,)),
        ],
        compiler_params=pltpu.CompilerParams(collective_id=2, has_side_effects=True),
        name="long_mixer",
    )(residual, edge, scale, gains, features, taps, jnp.asarray(forward), jnp.asarray(inverse))


def row_scale(row_power):
    other = lax.ppermute(row_power, "tp", [(0, 1), (1, 0)])
    return lax.rsqrt((row_power + other) / D + eps)


def scaled_rows(residual, scale_rows, gain_row):
    return settle(residual.astype(jnp.float32) * scale_rows[:, None] * gain_row)


def spread_kernel(count, mine_ref, all_ref, send_sem, recv_sem):
    me = lax.axis_index("seq")
    barrier = pltpu.get_barrier_semaphore()
    for step in range(1, count):
        peer = lax.rem(me + step, count)
        pl.semaphore_signal(barrier, inc=1, device_id={"seq": peer}, device_id_type=pl.DeviceIdType.MESH)
    pl.semaphore_wait(barrier, count - 1)
    copies = []
    for step in range(1, count):
        peer = lax.rem(me + step, count)
        copy = pltpu.make_async_remote_copy(
            src_ref=mine_ref,
            dst_ref=all_ref.at[me],
            send_sem=send_sem.at[step],
            recv_sem=recv_sem.at[step],
            device_id={"seq": peer},
            device_id_type=pl.DeviceIdType.MESH,
        )
        copy.start()
        copies.append(copy)
    all_ref[me] = mine_ref[...]
    for copy in copies:
        copy.wait()


def spread(value):
    count = lax.axis_size("seq")
    return pl.pallas_call(
        functools.partial(spread_kernel, count),
        out_shape=jax.ShapeDtypeStruct((count, *value.shape), value.dtype),
        in_specs=[pl.BlockSpec(memory_space=pltpu.VMEM)],
        out_specs=pl.BlockSpec(memory_space=pltpu.VMEM),
        scratch_shapes=[pltpu.SemaphoreType.DMA((count,)), pltpu.SemaphoreType.DMA((count,))],
        compiler_params=pltpu.CompilerParams(collective_id=0, has_side_effects=True),
        name="spread",
    )(value)


def shards(
    hidden,
    targets,
    perturb_sites,
    labels,
    norm_gain,
    feature_taps,
    short_taps,
    long_taps,
    head_weight,
):
    residual = hidden[0]
    row_count = residual.shape[0]
    short_back = FEAT_TAPS + SE_TAPS - 2
    long_back = FEAT_TAPS + MR_TAPS - 2
    long_lead = -(-long_back // 16) * 16
    widened = residual.astype(jnp.float32)
    scale_one = row_scale(jnp.sum(widened * widened, axis=1))
    last = row_count - short_back
    rim_rows = passed_along(scaled_rows(residual[last:], scale_one[last:], norm_gain[0]), "seq", 1)
    after_short, power_two, taps_all = short_mixer(
        residual, rim_rows, scale_one[:, None], norm_gain, feature_taps, short_taps, long_taps
    )
    scale_two = row_scale(jnp.sum(power_two, axis=1))
    last = row_count - long_lead
    edge_rows = scaled_rows(after_short[last:], scale_two[last:], norm_gain[1])
    after_long, power_three = long_mixer(
        after_short, edge_rows, scale_two[:, None], norm_gain, feature_taps, taps_all.reshape(MR_TAPS, -1)
    )
    final_norm = scaled_rows(after_long, row_scale(jnp.sum(power_three, axis=1)), norm_gain[2])
    row_contract = (((1,), (1,)), ((), ()))
    logits_part = lax.dot_general(
        final_norm,
        lax.all_gather(head_weight, ("seq", "fsdp"), axis=0, tiled=True),
        row_contract,
        preferred_element_type=jnp.float32,
    )
    core = lax.axis_index("tp")
    swap = [(0, 1), (1, 0)]
    half_rows = row_count // 2
    kept = lax.dynamic_slice_in_dim(logits_part, core * half_rows, half_rows, 0)
    given = lax.dynamic_slice_in_dim(logits_part, (1 - core) * half_rows, half_rows, 0)
    logits = kept + lax.ppermute(given, "tp", swap)
    row_peak = jnp.max(logits, axis=1, keepdims=True)
    log_total = jnp.log(jnp.sum(jnp.exp(logits - row_peak), axis=1)) + row_peak[:, 0]
    target_row = lax.dynamic_slice_in_dim(targets[0], core * half_rows, half_rows, 0)
    vocab_ids = lax.broadcasted_iota(jnp.int32, logits.shape, 1)
    chosen = jnp.sum(jnp.where(vocab_ids == target_row[:, None], logits, 0.0), axis=1)
    mine = chosen - log_total
    theirs = lax.ppermute(mine, "tp", swap)
    logprob = jnp.where(core == 0, jnp.concatenate([mine, theirs]), jnp.concatenate([theirs, mine]))
    site_row = perturb_sites[0]
    genome_row = spread(logprob.reshape(-1, 128)).reshape(-1)
    positions = lax.broadcasted_iota(jnp.int32, (site_row.shape[0], genome_row.shape[0]), 1)
    prefix_sum = jnp.sum(jnp.where(positions < site_row[:, None], genome_row[None, :], 0.0), axis=1)
    site_logprob = jnp.sum(jnp.where(positions == site_row[:, None], genome_row[None, :], 0.0), axis=1)
    prefix_len = jnp.maximum(site_row, 1).astype(jnp.float32)
    surprise = site_logprob - prefix_sum / prefix_len
    label_sign = (2 * labels[0] - 1).astype(jnp.float32)
    contrast = jnp.sum(label_sign * surprise) / (SITES // 2)
    return (logprob[None, :], surprise[None, :], jnp.reshape(contrast, (1,)))


def solution(mesh):
    placed = (
        P(("grp", "fsdp"), "seq", "tp"),
        P(("grp", "fsdp"), "seq"),
        P(("grp", "fsdp"), None),
        P(("grp", "fsdp"), None),
        P(None, "tp"),
        P(None, None, None, "tp"),
        P(None, "tp"),
        P(("seq", "fsdp"), "tp"),
        P(("seq", "fsdp"), "tp"),
    )
    return jax.shard_map(
        shards,
        mesh=mesh,
        in_specs=placed,
        out_specs=(P(("grp", "fsdp"), "seq"), P(("grp", "fsdp"), None), P(("grp", "fsdp"))),
        check_vma=False,
    )
```

```python
import functools

import jax
import jax.numpy as jnp
import numpy as np
from jax import lax
from jax.experimental import pallas as pl
from jax.experimental.pallas import tpu as pltpu
from jax.sharding import PartitionSpec as P

D = 8192
FEAT_TAPS = 3
SE_TAPS = 7
MR_TAPS = 128
SITES = 64


eps = 1e-06


def passed_along(shard, axis, by):
    devices = lax.axis_size(axis)
    pairs = [(i, i + by) for i in range(devices) if 0 <= i + by < devices]
    return lax.ppermute(shard, axis, pairs)


def settle(tensor):
    return lax.optimization_barrier(tensor.astype(jnp.bfloat16))


def split_parts(matrix, parts):
    pieces, left = [], np.asarray(matrix, np.float64)
    for _ in range(parts):
        piece = left.astype(jnp.bfloat16)
        pieces.append(piece)
        left = left - piece.astype(np.float64)
    return np.stack(pieces)


def transform_pair(window, taps):
    half = window // 2
    t = np.arange(window)
    f = np.arange(half)
    angle = 2.0 * np.pi * ((f[:, None] * t[None, :]) % window) / window
    cos_rows, sin_rows = np.cos(angle), np.sin(angle)
    sin_rows[0] = np.where(t % 2 == 0, 1.0, -1.0)
    forward = np.concatenate([cos_rows, sin_rows], axis=0)
    weight = np.full((half,), 2.0 / window)
    weight[0] = 1.0 / window
    inverse = (forward * np.concatenate([weight, weight])[:, None]).T[taps:]
    return split_parts(forward, PARTS), split_parts(inverse, PARTS)


PARTS = 3
CHUNK = 32
WIDTH = 256


def wide(value):
    return value.astype(jnp.float32)


def rounded(value):
    return value.astype(jnp.bfloat16).astype(jnp.float32)


def tap_sum(ref, start, rows, taps):
    total = taps[0] * ref[start : start + rows, :]
    for lag in range(1, len(taps)):
        total = total + taps[lag] * ref[start - lag : start - lag + rows, :]
    return total


def tap_rows(taps):
    taps = wide(taps)
    return [taps[lag : lag + 1, :] for lag in range(taps.shape[0])]


def feature_rows(feat_ref, which):
    return tap_rows(feat_ref[0, which])


def square_lanes(value):
    square = value * value
    total = square[:, :128]
    for at in range(128, square.shape[1], 128):
        total = total + square[:, at : at + 128]
    return total


def gather_peer(step, counts):
    outer, inner = counts
    place = lax.rem(lax.axis_index("seq") * inner + lax.axis_index("fsdp") + step, outer * inner)
    return place, {"seq": place // inner, "fsdp": lax.rem(place, inner)}


def short_kernel(
    counts, hid_ref, rim_ref, scale_ref, gain_ref, feat_ref, taps_ref, piece_ref,
    out_ref, pow_ref, whole_ref, ext, inner, send_sem, recv_sem, own_sem,
):
    rows = hid_ref.shape[0]
    lead = rim_ref.shape[0]
    holders = counts[0] * counts[1]
    mine, _ = gather_peer(0, counts)

    def to_peer(step):
        _, where = gather_peer(step, counts)
        return pltpu.make_async_remote_copy(
            src_ref=piece_ref,
            dst_ref=whole_ref.at[mine],
            send_sem=send_sem.at[step],
            recv_sem=recv_sem.at[step],
            device_id=where,
            device_id_type=pl.DeviceIdType.MESH,
        )

    own_copy = pltpu.make_async_copy(piece_ref, whole_ref.at[mine], own_sem)

    @pl.when(pl.program_id(0) == 0)
    def _():
        pow_ref[...] = jnp.zeros_like(pow_ref)
        barrier = pltpu.get_barrier_semaphore()

        def greet(step, carry):
            _, where = gather_peer(step, counts)
            pl.semaphore_signal(barrier, inc=1, device_id=where, device_id_type=pl.DeviceIdType.MESH)
            return carry

        def send(step, carry):
            to_peer(step).start()
            return carry

        lax.fori_loop(1, holders, greet, 0)
        pl.semaphore_wait(barrier, holders - 1)
        lax.fori_loop(1, holders, send, 0)
        own_copy.start()

    @pl.when(pl.program_id(0) == pl.num_programs(0) - 1)
    def _():
        def settle_copy(step, carry):
            to_peer(step).wait()
            return carry

        lax.fori_loop(1, holders, settle_copy, 0)
        own_copy.wait()

    ext[0:lead, :] = jnp.zeros((lead, ext.shape[1]), jnp.float32)
    ext[lead : 2 * lead, :] = wide(rim_ref[...])
    gain = gain_ref[0:1, :]
    for at in range(0, rows, CHUNK):
        block = wide(hid_ref[at : at + CHUNK, :])
        ext[2 * lead + at : 2 * lead + at + CHUNK, :] = rounded(block * scale_ref[at : at + CHUNK, :] * gain)
    k_taps, v_taps = feature_rows(feat_ref, 1), feature_rows(feat_ref, 2)

    def inner_rows(at, count):
        keys = rounded(tap_sum(ext, lead + at, count, k_taps))
        values = rounded(tap_sum(ext, lead + at, count, v_taps))
        inner[at : at + count, :] = rounded(keys * values)

    inner_rows(0, lead)
    for at in range(0, rows, CHUNK):
        inner_rows(lead + at, CHUNK)
    q_taps = feature_rows(feat_ref, 0)
    short = tap_rows(taps_ref[...])
    for at in range(0, rows, CHUNK):
        queries = rounded(tap_sum(ext, 2 * lead + at, CHUNK, q_taps))
        filtered = tap_sum(inner, lead + at, CHUNK, short)
        result = (wide(hid_ref[at : at + CHUNK, :]) + queries * filtered).astype(jnp.bfloat16)
        out_ref[at : at + CHUNK, :] = result
        pow_ref[at : at + CHUNK, :] += square_lanes(wide(result))


def short_mixer(residual, rim, scale, gains, features, taps, piece):
    rows, channels = residual.shape
    lead = rim.shape[0]
    counts = (lax.axis_size("seq"), lax.axis_size("fsdp"))
    holders = counts[0] * counts[1]
    column = lambda i: (0, i)
    fixed = lambda i: (0, 0)
    return pl.pallas_call(
        functools.partial(short_kernel, counts),
        grid=(channels // WIDTH,),
        in_specs=[
            pl.BlockSpec((rows, WIDTH), column),
            pl.BlockSpec((lead, WIDTH), column),
            pl.BlockSpec((rows, 1), fixed),
            pl.BlockSpec((gains.shape[0], WIDTH), column),
            pl.BlockSpec((1, *features.shape[1:3], WIDTH), lambda i: (0, 0, 0, i)),
            pl.BlockSpec((taps.shape[0], WIDTH), column),
            pl.BlockSpec(memory_space=pl.ANY),
        ],
        out_specs=[
            pl.BlockSpec((rows, WIDTH), column),
            pl.BlockSpec((rows, 128), fixed),
            pl.BlockSpec(memory_space=pl.ANY),
        ],
        out_shape=[
            jax.ShapeDtypeStruct((rows, channels), jnp.bfloat16),
            jax.ShapeDtypeStruct((rows, 128), jnp.float32),
            jax.ShapeDtypeStruct((holders, *piece.shape), piece.dtype),
        ],
        scratch_shapes=[
            pltpu.VMEM((2 * lead + rows, WIDTH), jnp.float32),
            pltpu.VMEM((lead + rows, WIDTH), jnp.float32),
            pltpu.SemaphoreType.DMA((holders,)),
            pltpu.SemaphoreType.DMA((holders,)),
            pltpu.SemaphoreType.DMA,
        ],
        compiler_params=pltpu.CompilerParams(collective_id=1, has_side_effects=True),
        name="short_mixer",
    )(residual, rim, scale, gains, features, taps, piece)


def long_kernel(
    count, res_ref, edge_ref, scale_ref, gain_ref, feat_ref, taps_ref, fwd_ref, inv_ref,
    out_ref, pow_ref, ext, inner, spec_u, spec_w, spec_y, filt, rim, send_sem, recv_sem,
):
    rows = res_ref.shape[0]
    tap_count = taps_ref.shape[0]
    lead = rim.shape[1]
    step = pl.program_id(0)
    blocks = pl.num_programs(0)
    me = lax.axis_index("seq")
    sends, receives = me < count - 1, me > 0

    def onward(block):
        return pltpu.make_async_remote_copy(
            src_ref=edge_ref.at[:, pl.ds(pl.multiple_of(block * WIDTH, WIDTH), WIDTH)],
            dst_ref=rim.at[block],
            send_sem=send_sem.at[block],
            recv_sem=recv_sem.at[block],
            device_id={"seq": lax.rem(me + 1, count)},
            device_id_type=pl.DeviceIdType.MESH,
        )

    @pl.when(step == 0)
    def _():
        barrier = pltpu.get_barrier_semaphore()

        @pl.when(receives)
        def _():
            pl.semaphore_signal(barrier, inc=1, device_id={"seq": me - 1}, device_id_type=pl.DeviceIdType.MESH)

        @pl.when(sends)
        def _():
            pl.semaphore_signal(barrier, inc=1, device_id={"seq": me + 1}, device_id_type=pl.DeviceIdType.MESH)

        between = jnp.logical_and(receives, sends)

        @pl.when(between)
        def _():
            pl.semaphore_wait(barrier, 2)

        @pl.when(jnp.logical_not(between))
        def _():
            pl.semaphore_wait(barrier, 1)

        @pl.when(sends)
        def _():
            def send(block, carry):
                onward(block).start()
                return carry

            lax.fori_loop(0, blocks, send, 0)

    @pl.when(receives)
    def _():
        onward(step).wait_recv()
        ext[0:lead, :] = wide(rim[step])

    @pl.when(jnp.logical_not(receives))
    def _():
        ext[0:lead, :] = jnp.zeros((lead, ext.shape[1]), jnp.float32)

    @pl.when(sends)
    def _():
        onward(step).wait_send()

    window = tap_count + rows
    half = window // 2

    @pl.when(pl.program_id(0) == 0)
    def _():
        pow_ref[...] = jnp.zeros_like(pow_ref)

    gain = gain_ref[1:2, :]
    for at in range(0, rows, CHUNK):
        block = wide(res_ref[at : at + CHUNK, :])
        ext[lead + at : lead + at + CHUNK, :] = rounded(block * scale_ref[at : at + CHUNK, :] * gain)
    k_taps, v_taps = feature_rows(feat_ref, 1), feature_rows(feat_ref, 2)
    first = lead - tap_count
    for at in range(0, window, CHUNK):
        keys = rounded(tap_sum(ext, first + at, CHUNK, k_taps))
        values = rounded(tap_sum(ext, first + at, CHUNK, v_taps))
        inner[at : at + CHUNK, :] = (keys * values).astype(jnp.bfloat16)

    def product(left, right):
        return jnp.dot(left, right, preferred_element_type=jnp.float32)

    def forward_of(value, depth):
        total = product(fwd_ref[PARTS - 1][:, :depth], value)
        for part in range(PARTS - 2, -1, -1):
            total = total + product(fwd_ref[part][:, :depth], value)
        return total

    taps = taps_ref[...]
    signal = inner[...]
    spec_w[...] = forward_of(taps, tap_count)
    spec_u[...] = forward_of(signal, window)
    for at in range(0, half, CHUNK):
        lo, hi = slice(at, at + CHUNK), slice(half + at, half + at + CHUNK)
        uc, us, wc, ws = spec_u[lo, :], spec_u[hi, :], spec_w[lo, :], spec_w[hi, :]
        cc, ss = uc * wc, us * ws
        yc, ys = cc - ss, uc * ws + us * wc
        if at == 0:
            is_first = lax.broadcasted_iota(jnp.int32, cc.shape, 0) == 0
            yc, ys = jnp.where(is_first, cc, yc), jnp.where(is_first, ss, ys)
        for rows_at, value in ((lo, yc), (hi, ys)):
            for part in range(PARTS):
                top = value.astype(jnp.bfloat16)
                spec_y[part, rows_at, :] = top
                value = value - wide(top)
    total = None
    for order in range(PARTS - 1, -1, -1):
        for part in range(order + 1):
            term = product(inv_ref[part], spec_y[order - part])
            total = term if total is None else total + term
    filt[...] = total
    q_taps = feature_rows(feat_ref, 0)
    for at in range(0, rows, CHUNK):
        queries = rounded(tap_sum(ext, lead + at, CHUNK, q_taps))
        result = (wide(res_ref[at : at + CHUNK, :]) + queries * filt[at : at + CHUNK, :]).astype(jnp.bfloat16)
        out_ref[at : at + CHUNK, :] = result
        pow_ref[at : at + CHUNK, :] += square_lanes(wide(result))


def long_mixer(residual, edge, scale, gains, features, taps):
    rows, channels = residual.shape
    lead, tap_count = edge.shape[0], taps.shape[0]
    count, blocks = lax.axis_size("seq"), channels // WIDTH
    window = rows + tap_count
    forward, inverse = transform_pair(window, tap_count)
    column = lambda i: (0, i)
    fixed = lambda i: (0, 0)
    whole = lambda i: (0, 0, 0)
    return pl.pallas_call(
        functools.partial(long_kernel, count),
        grid=(channels // WIDTH,),
        in_specs=[
            pl.BlockSpec((rows, WIDTH), column),
            pl.BlockSpec(memory_space=pl.ANY),
            pl.BlockSpec((rows, 1), fixed),
            pl.BlockSpec((gains.shape[0], WIDTH), column),
            pl.BlockSpec((1, *features.shape[1:3], WIDTH), lambda i: (1, 0, 0, i)),
            pl.BlockSpec((tap_count, WIDTH), column),
            pl.BlockSpec(forward.shape, whole),
            pl.BlockSpec(inverse.shape, whole),
        ],
        out_specs=[pl.BlockSpec((rows, WIDTH), column), pl.BlockSpec((rows, 128), fixed)],
        out_shape=[
            jax.ShapeDtypeStruct((rows, channels), jnp.bfloat16),
            jax.ShapeDtypeStruct((rows, 128), jnp.float32),
        ],
        scratch_shapes=[
            pltpu.VMEM((lead + rows, WIDTH), jnp.float32),
            pltpu.VMEM((window, WIDTH), jnp.bfloat16),
            pltpu.VMEM((window, WIDTH), jnp.float32),
            pltpu.VMEM((window, WIDTH), jnp.float32),
            pltpu.VMEM((PARTS, window, WIDTH), jnp.bfloat16),
            pltpu.VMEM((rows, WIDTH), jnp.float32),
            pltpu.VMEM((blocks, lead, WIDTH), jnp.bfloat16),
            pltpu.SemaphoreType.DMA((blocks,)),
            pltpu.SemaphoreType.DMA((blocks,)),
        ],
        compiler_params=pltpu.CompilerParams(collective_id=2, has_side_effects=True),
        cost_estimate=pl.CostEstimate(flops=12 * window * window * channels, bytes_accessed=8 * rows * channels, transcendentals=0),
        name="long_mixer",
    )(residual, edge, scale, gains, features, taps, jnp.asarray(forward), jnp.asarray(inverse))


def row_scale(row_power):
    other = lax.ppermute(row_power, "tp", [(0, 1), (1, 0)])
    return lax.rsqrt((row_power + other) / D + eps)


def scaled_rows(residual, scale_rows, gain_row):
    return settle(residual.astype(jnp.float32) * scale_rows[:, None] * gain_row)


def spread_kernel(count, mine_ref, all_ref, send_sem, recv_sem):
    me = lax.axis_index("seq")
    barrier = pltpu.get_barrier_semaphore()
    for step in range(1, count):
        peer = lax.rem(me + step, count)
        pl.semaphore_signal(barrier, inc=1, device_id={"seq": peer}, device_id_type=pl.DeviceIdType.MESH)
    pl.semaphore_wait(barrier, count - 1)
    copies = []
    for step in range(1, count):
        peer = lax.rem(me + step, count)
        copy = pltpu.make_async_remote_copy(
            src_ref=mine_ref,
            dst_ref=all_ref.at[me],
            send_sem=send_sem.at[step],
            recv_sem=recv_sem.at[step],
            device_id={"seq": peer},
            device_id_type=pl.DeviceIdType.MESH,
        )
        copy.start()
        copies.append(copy)
    all_ref[me] = mine_ref[...]
    for copy in copies:
        copy.wait()


def spread(value):
    count = lax.axis_size("seq")
    return pl.pallas_call(
        functools.partial(spread_kernel, count),
        out_shape=jax.ShapeDtypeStruct((count, *value.shape), value.dtype),
        in_specs=[pl.BlockSpec(memory_space=pltpu.VMEM)],
        out_specs=pl.BlockSpec(memory_space=pltpu.VMEM),
        scratch_shapes=[pltpu.SemaphoreType.DMA((count,)), pltpu.SemaphoreType.DMA((count,))],
        compiler_params=pltpu.CompilerParams(collective_id=0, has_side_effects=True),
        name="spread",
    )(value)


def shards(
    hidden,
    targets,
    perturb_sites,
    labels,
    norm_gain,
    feature_taps,
    short_taps,
    long_taps,
    head_weight,
):
    residual = hidden[0]
    row_count = residual.shape[0]
    short_back = FEAT_TAPS + SE_TAPS - 2
    long_back = FEAT_TAPS + MR_TAPS - 2
    long_lead = -(-long_back // 16) * 16
    widened = residual.astype(jnp.float32)
    scale_one = row_scale(jnp.sum(widened * widened, axis=1))
    last = row_count - short_back
    rim_rows = passed_along(scaled_rows(residual[last:], scale_one[last:], norm_gain[0]), "seq", 1)
    after_short, power_two, taps_all = short_mixer(
        residual, rim_rows, scale_one[:, None], norm_gain, feature_taps, short_taps, long_taps
    )
    scale_two = row_scale(jnp.sum(power_two, axis=1))
    last = row_count - long_lead
    edge_rows = scaled_rows(after_short[last:], scale_two[last:], norm_gain[1])
    part, parts = lax.axis_index("grp"), lax.axis_size("grp")
    slab = head_weight.shape[0] // parts
    own_slab = lax.dynamic_slice_in_dim(head_weight, part * slab, slab, 0)
    head_own = lax.all_gather(own_slab, ("seq", "fsdp"), axis=0, tiled=True)
    taps_all, head_own = lax.optimization_barrier((taps_all, head_own))
    heads = [head_own]
    for turn in range(1, parts):
        heads.append(lax.ppermute(head_own, "grp", [(i, (i + turn) % parts) for i in range(parts)]))
    after_long, power_three = long_mixer(
        after_short, edge_rows, scale_two[:, None], norm_gain, feature_taps, taps_all.reshape(MR_TAPS, -1)
    )
    final_norm = scaled_rows(after_long, row_scale(jnp.sum(power_three, axis=1)), norm_gain[2])
    row_contract = (((1,), (1,)), ((), ()))
    logits_part = jnp.concatenate(
        [lax.dot_general(final_norm, head, row_contract, preferred_element_type=jnp.float32) for head in heads], axis=1
    )
    core = lax.axis_index("tp")
    swap = [(0, 1), (1, 0)]
    half_rows = row_count // 2
    kept = lax.dynamic_slice_in_dim(logits_part, core * half_rows, half_rows, 0)
    given = lax.dynamic_slice_in_dim(logits_part, (1 - core) * half_rows, half_rows, 0)
    logits = kept + lax.ppermute(given, "tp", swap)
    row_peak = jnp.max(logits, axis=1, keepdims=True)
    log_total = jnp.log(jnp.sum(jnp.exp(logits - row_peak), axis=1)) + row_peak[:, 0]
    target_row = lax.dynamic_slice_in_dim(targets[0], core * half_rows, half_rows, 0)
    column = lax.broadcasted_iota(jnp.int32, logits.shape, 1)
    section = head_own.shape[0]
    from_part = lax.rem(part + parts - column // section, parts)
    within = lax.rem(column, section)
    vocab_ids = (within // slab) * head_weight.shape[0] + from_part * slab + lax.rem(within, slab)
    chosen = jnp.sum(jnp.where(vocab_ids == target_row[:, None], logits, 0.0), axis=1)
    mine = chosen - log_total
    theirs = lax.ppermute(mine, "tp", swap)
    logprob = jnp.where(core == 0, jnp.concatenate([mine, theirs]), jnp.concatenate([theirs, mine]))
    site_row = perturb_sites[0]
    genome_row = spread(logprob.reshape(-1, 128)).reshape(-1)
    positions = lax.broadcasted_iota(jnp.int32, (site_row.shape[0], genome_row.shape[0]), 1)
    prefix_sum = jnp.sum(jnp.where(positions < site_row[:, None], genome_row[None, :], 0.0), axis=1)
    site_logprob = jnp.sum(jnp.where(positions == site_row[:, None], genome_row[None, :], 0.0), axis=1)
    prefix_len = jnp.maximum(site_row, 1).astype(jnp.float32)
    surprise = site_logprob - prefix_sum / prefix_len
    label_sign = (2 * labels[0] - 1).astype(jnp.float32)
    contrast = jnp.sum(label_sign * surprise) / (SITES // 2)
    return (logprob[None, :], surprise[None, :], jnp.reshape(contrast, (1,)))


def solution(mesh):
    placed = (
        P(("grp", "fsdp"), "seq", "tp"),
        P(("grp", "fsdp"), "seq"),
        P(("grp", "fsdp"), None),
        P(("grp", "fsdp"), None),
        P(None, "tp"),
        P(None, None, None, "tp"),
        P(None, "tp"),
        P(("seq", "fsdp"), "tp"),
        P(("seq", "fsdp"), "tp"),
    )
    return jax.shard_map(
        shards,
        mesh=mesh,
        in_specs=placed,
        out_specs=(P(("grp", "fsdp"), "seq"), P(("grp", "fsdp"), None), P(("grp", "fsdp"))),
        check_vma=False,
    )
```
